32 devices in a mesh: dp: 8 (over z, core), mp: 4 (over y, x).
Axes of the slice: x: 2, y: 2, z: 4, core: 2. Of those that a mesh axis runs over, the one named last changes fastest.
Arguments:
- stream: bfloat16 [1152, 2640], P('dp'), may hold values from -6 to 6
- embedding: bfloat16 [1152, 2640], P('dp'), may hold values from -6 to 6
- cotangent: bfloat16 [1152, 2640], P('dp'), may hold values from -6 to 6
- norm_gain: float32 [2640], replicated, may hold values from 0.1 to 1.9
- up_weight: bfloat16 [2640, 8960], P('dp', 'mp'), may hold values from -0.125 to 0.125
- down_weight: bfloat16 [8960, 2640], P('mp', 'dp'), may hold values from -0.0625 to 0.0625
- counts: int32 [384], P('dp'), may hold values from 0 to 2, as said below
- destination: int32 [384], P('dp'), may hold values from 0 to 383, as said below
Outputs:
- new_stream: bfloat16 [1152, 2640], P('dp')
- embed_grad: bfloat16 [1152, 2640], P('dp')
The draws below stay inside these ranges and needn't reach their ends.
Inputs may be any that keep to these rules, and one draw needn't show every extreme that they name: `counts`: A quarter of the indices of dp hold only blocks with a positive count; every other index holds 16 such blocks. `destination`: A permutation of the 384 block positions. Every index of dp sends the same number of blocks to every index of dp (a position p belongs to index p // 48), and exactly 24 blocks with a positive count are sent to each index.
All inputs are finite; a program needn't handle non-finite values.
Results may differ from the reference program's by a relative error of at most 0.02.
Values may be sent and summed in bfloat16 or wider, within the bound.
A program may use at most 128 MiB of HBM per device.

```python
import jax
import jax.numpy as jnp
from jax import lax

D = 2640
FF = 8960
BR = 3
NB = 48
BLOCKS = 384
TOKENS = 1152
PART = 2240
N_MP = 4


def routing_plan(key):
    folded = jax.random.fold_in(key, 7)
    subkeys = jax.random.split(folded, 6)
    devices = BLOCKS // NB
    quiet_load = NB // 3
    quarter = devices // 4
    profile = jnp.where(jnp.arange(devices) < quarter, NB, quiet_load).astype(jnp.int32)
    live_load = profile[jax.random.permutation(subkeys[0], devices)]
    orders = jax.vmap(lambda subkey: jax.random.permutation(subkey, NB))(jax.random.split(subkeys[1], devices))
    local_rank = jnp.argsort(orders, axis=1, stable=True).astype(jnp.int32)
    active = local_rank < live_load[:, None]
    levels = jax.random.randint(subkeys[2], (devices, NB), 1, 3)
    counts = jnp.where(active, levels, 0).astype(jnp.int32)
    first_rank = jnp.cumsum(live_load) - live_load
    offset = jax.random.randint(subkeys[3], (), 0, devices)
    relabel = jax.random.permutation(subkeys[4], devices)
    cyclic = (first_rank[:, None] + local_rank + offset) % devices
    target = relabel[cyclic]
    within = jnp.arange(devices)[:, None] * (NB // devices) + local_rank // devices
    shuffles = jax.vmap(lambda subkey: jax.random.permutation(subkey, NB))(jax.random.split(subkeys[5], devices))
    dest_slot = shuffles[target, within]
    destination = (target * NB + dest_slot).astype(jnp.int32)
    return (counts.reshape(BLOCKS), destination.reshape(BLOCKS))


def draw_counts(key, part):
    return routing_plan(key)[0]


def draw_destination(key, part):
    return routing_plan(key)[1]


def block_scale(own_key, dims, cuts, least, top_value):
    level, own = 1.0, jax.random.fold_in(own_key, 6)
    for axis_at, parts in cuts:
        steps = jnp.exp(jax.random.uniform(jax.random.fold_in(own, axis_at), (parts,), jnp.float32, least / len(cuts), top_value / len(cuts)))
        level = level * jnp.repeat(steps, dims[axis_at] // parts).reshape([-1 if axis == axis_at else 1 for axis in range(len(dims))])
    return level


def normal_values(key, shape, scale, reach, shards=(), held_as=jnp.bfloat16):
    result = scale * jax.random.normal(key, shape, jnp.float32)
    if shards:
        result = result * block_scale(key, shape, shards, -0.22, 0.18)
    return jnp.clip(result, -reach, reach).astype(held_as)


def setup_inputs(seed: int = 0) -> dict:
    key_of = jax.random.split(jax.random.key(seed), 9)
    stream = normal_values(key_of[0], (TOKENS, D), 1.0, 6.0, ((0, 8),))
    embedding = normal_values(key_of[1], (TOKENS, D), 1.0, 6.0, ((0, 8),))
    cotangent = normal_values(key_of[2], (TOKENS, D), 1.0, 6.0, ((0, 8),))
    norm_gain = jnp.clip(1.0 + 0.18 * jax.random.normal(key_of[3], (D,), jnp.float32), 0.1, 1.9)
    up_weight = normal_values(key_of[4], (D, FF), D ** -0.5, 0.125, ((0, 8), (1, 4)))
    down_weight = normal_values(key_of[5], (FF, D), FF ** -0.5, 0.0625, ((0, 4), (1, 8)))
    counts = draw_counts(jax.random.fold_in(key_of[8], 71), 0)
    destination = draw_destination(jax.random.fold_in(key_of[8], 71), 0)
    return dict(stream=stream, embedding=embedding, cotangent=cotangent, norm_gain=norm_gain, up_weight=up_weight, down_weight=down_weight, counts=counts, destination=destination)


EPSILON = 1e-05

def layer_input(current, embedding, norm_gain):
    values = current.astype(jnp.float32)
    square = lax.optimization_barrier(jnp.mean(values * values, axis=-1, keepdims=True))
    mixed = values * lax.rsqrt(square + EPSILON) * norm_gain + embedding.astype(jnp.float32)
    return mixed.astype(jnp.bfloat16)

def rounded_part(value):
    return lax.optimization_barrier(value.astype(jnp.bfloat16)).astype(jnp.float32)

def reference(stream, embedding, cotangent, norm_gain, up_weight, down_weight, counts, destination):
    row_counts = jnp.repeat(counts, BR)
    current = stream
    pre_last = jnp.zeros((TOKENS, FF), jnp.float32)
    for iteration in range(2):
        layer_in = layer_input(current, embedding, norm_gain)
        pre_act = jnp.dot(layer_in, up_weight, preferred_element_type=jnp.float32)
        activation = jax.nn.silu(pre_act).astype(jnp.bfloat16)
        update = jnp.zeros((TOKENS, D), jnp.float32)
        for piece in range(N_MP):
            lower = piece * PART
            product = jnp.dot(activation[:, lower:lower + PART], down_weight[lower:lower + PART, :], preferred_element_type=jnp.float32)
            update = update + rounded_part(product)
        advanced = (current.astype(jnp.float32) + update).astype(jnp.bfloat16)
        current = jnp.where((row_counts > iteration)[:, None], advanced, current)
        pre_last = pre_act
    cot_source = cotangent.reshape(BLOCKS, BR * D)[destination].reshape(TOKENS, D)
    grad_act = jnp.dot(cot_source, down_weight.T, preferred_element_type=jnp.float32)
    sigmoid_pre = jax.nn.sigmoid(pre_last)
    grad_pre = (grad_act * (sigmoid_pre * (1.0 + pre_last * (1.0 - sigmoid_pre)))).astype(jnp.bfloat16)
    grad_input = jnp.zeros((TOKENS, D), jnp.float32)
    for piece in range(N_MP):
        lower = piece * PART
        product = jnp.dot(grad_pre[:, lower:lower + PART], up_weight[:, lower:lower + PART].T, preferred_element_type=jnp.float32)
        grad_input = grad_input + rounded_part(product)
    grads = jnp.where((row_counts > 1)[:, None], grad_input, 0.0).astype(jnp.bfloat16)
    new_stream = jnp.zeros((BLOCKS, BR * D), jnp.bfloat16).at[destination].set(current.reshape(BLOCKS, BR * D))
    embed_grad = jnp.zeros((BLOCKS, BR * D), jnp.bfloat16).at[destination].set(grads.reshape(BLOCKS, BR * D))
    return (new_stream.reshape(TOKENS, D), embed_grad.reshape(TOKENS, D))
```

```python
import functools

import jax
import jax.numpy as jnp
from jax import lax
from jax.experimental import pallas as pl
from jax.experimental.pallas import tpu as pltpu
from jax.sharding import PartitionSpec as P

EPSILON = 1e-05
MESH = pl.DeviceIdType.MESH


def sum_kernel(n, part_ref, out_ref, got, full, send_sem, recv_sem, share_sem, full_sem):
    me = lax.axis_index("mp")
    barrier = pltpu.get_barrier_semaphore()
    for k in range(1, n):
        peer = lax.rem(me + k, n)
        pl.semaphore_signal(barrier, inc=1, device_id={"mp": peer}, device_id_type=MESH)
    pl.semaphore_wait(barrier, n - 1)
    scatter = []
    for k in range(1, n):
        peer = lax.rem(me + k, n)
        scatter.append(
            pltpu.make_async_remote_copy(
                src_ref=part_ref.at[peer],
                dst_ref=got.at[k],
                send_sem=send_sem.at[k],
                recv_sem=recv_sem.at[k],
                device_id={"mp": peer},
                device_id_type=MESH,
            )
        )
        scatter[-1].start()
    total = part_ref[me].astype(jnp.float32)
    for k in range(1, n):
        scatter[k - 1].wait_recv()
        total = total + got[k].astype(jnp.float32)
    full[0] = total.astype(full.dtype)
    share = []
    for k in range(1, n):
        peer = lax.rem(me + k, n)
        share.append(
            pltpu.make_async_remote_copy(
                src_ref=full.at[0],
                dst_ref=full.at[k],
                send_sem=share_sem.at[k],
                recv_sem=full_sem.at[k],
                device_id={"mp": peer},
                device_id_type=MESH,
            )
        )
        share[-1].start()
    out_ref[me] = full[0]
    for k in range(1, n):
        share[k - 1].wait_recv()
        out_ref[lax.rem(me + n - k, n)] = full[k]
    for k in range(1, n):
        scatter[k - 1].wait_send()
        share[k - 1].wait_send()


def sum_over_mp(value, collective_id):
    n = lax.axis_size("mp")
    rows, width = value.shape
    if n == 1:
        return value
    each = -(-rows // n)
    padded = jnp.pad(value, ((0, each * n - rows), (0, 0))) if each * n != rows else value
    shape = (n, each, width)
    vmem = pl.BlockSpec(memory_space=pltpu.VMEM)
    out = pl.pallas_call(
        functools.partial(sum_kernel, n),
        out_shape=jax.ShapeDtypeStruct(shape, value.dtype),
        in_specs=[vmem],
        out_specs=vmem,
        scratch_shapes=[pltpu.VMEM(shape, value.dtype)] * 2 + [pltpu.SemaphoreType.DMA((n,))] * 4,
        compiler_params=pltpu.CompilerParams(collective_id=collective_id, has_side_effects=True),
    )(padded.reshape(shape))
    return out.reshape(each * n, width)[:rows]


def chunked(value, parts):
    return value.reshape(value.shape[0], parts, value.shape[1] // parts)


def times_up(value, up_parts):
    return jnp.einsum(
        "rpk,pkf->rf", chunked(value, up_parts.shape[0]), up_parts,
        preferred_element_type=jnp.float32,
    )


def times_up_transposed(value, up_parts):
    out = jnp.einsum("rf,pkf->rpk", value, up_parts, preferred_element_type=jnp.float32)
    return out.astype(jnp.bfloat16).reshape(value.shape[0], -1)


def times_down(value, down_parts):
    return times_up_transposed(value, down_parts)


def times_down_transposed(value, down_parts):
    return times_up(value, down_parts)


def layer_input(current, embedding, norm_gain):
    values = current.astype(jnp.float32)
    square = jnp.mean(values * values, axis=-1, keepdims=True)
    mixed = values * lax.rsqrt(square + EPSILON) * norm_gain + embedding.astype(jnp.float32)
    return mixed.astype(jnp.bfloat16)


def run_core(current, embedding, cot_rows, row_counts, norm_gain, up_parts, down_parts):
    grad_act = times_down_transposed(cot_rows, down_parts)
    layer_in = layer_input(current, embedding, norm_gain)
    activation = jax.nn.silu(times_up(layer_in, up_parts)).astype(jnp.bfloat16)
    activation = lax.optimization_barrier(activation)
    update = sum_over_mp(times_down(activation, down_parts), 0).astype(jnp.float32)
    advanced = (current.astype(jnp.float32) + update).astype(jnp.bfloat16)
    current = jnp.where((row_counts > 0)[:, None], advanced, current)
    layer_in = layer_input(current, embedding, norm_gain)
    pre_last = times_up(layer_in, up_parts)
    activation = jax.nn.silu(pre_last).astype(jnp.bfloat16)
    sigmoid_pre = jax.nn.sigmoid(pre_last)
    grad_act = lax.optimization_barrier(grad_act)
    grad_pre = (grad_act * (sigmoid_pre * (1.0 + pre_last * (1.0 - sigmoid_pre)))).astype(
        jnp.bfloat16
    )
    both = jnp.concatenate(
        [times_down(activation, down_parts), times_up_transposed(grad_pre, up_parts)], axis=0
    )
    both = sum_over_mp(both, 1)
    update, summed = both[: current.shape[0]], both[current.shape[0] :]
    advanced = (current.astype(jnp.float32) + update.astype(jnp.float32)).astype(jnp.bfloat16)
    last = (row_counts > 1)[:, None]
    return jnp.where(last, advanced, current), jnp.where(last, summed, jnp.zeros_like(summed))


def take_blocks(selector, block_data):
    return jnp.dot(
        selector.astype(jnp.bfloat16), block_data, preferred_element_type=jnp.float32
    ).astype(jnp.bfloat16)


def take_numbers(selector, numbers):
    return jnp.sum(jnp.where(selector, numbers[None, :], 0), axis=1).astype(jnp.int32)


def shards(stream, embedding, cotangent, norm_gain, up_weight, down_weight, counts, destination):
    up_parts = lax.all_gather(up_weight, "dp", axis=0, tiled=False)
    down_parts = lax.all_gather(down_weight.T, "dp", axis=0, tiled=False)
    row_total, feature_count = stream.shape
    blocks = counts.shape[0]
    block_rows = row_total // blocks
    block_width = block_rows * feature_count
    peer_count = lax.axis_size("dp")
    per_peer = blocks // peer_count
    peer_width = per_peer * block_width
    numbered = jnp.arange(blocks, dtype=jnp.int32)
    target = destination // blocks
    dest_slot = destination % blocks
    same_target = target[:, None] == target[None, :]
    earlier = numbered[None, :] < numbered[:, None]
    peer_rank = jnp.sum(same_target & earlier, axis=1)
    position = target * per_peer + peer_rank
    send_pick = position[None, :] == numbered[:, None]
    sent_slot = take_numbers(send_pick, dest_slot)
    stream_blocks = stream.reshape(blocks, block_width)
    embed_blocks = embedding.reshape(blocks, block_width)
    cot_blocks = cotangent.reshape(blocks, block_width)
    sent_count = take_numbers(send_pick, counts)
    sent_stream = take_blocks(send_pick, stream_blocks).reshape(peer_count, peer_width)
    sent_embed = take_blocks(send_pick, embed_blocks).reshape(peer_count, peer_width)
    got_stream, got_embed, got_count, got_slot = (
        lax.all_to_all(sent_stream, "dp", split_axis=0, concat_axis=0, tiled=True),
        lax.all_to_all(sent_embed, "dp", split_axis=0, concat_axis=0, tiled=True),
        lax.all_to_all(
            sent_count.reshape(peer_count, per_peer), "dp", split_axis=0, concat_axis=0, tiled=True
        ),
        lax.all_to_all(
            sent_slot.reshape(peer_count, per_peer), "dp", split_axis=0, concat_axis=0, tiled=True
        ),
    )
    got_stream = got_stream.reshape(blocks, block_width)
    got_embed = got_embed.reshape(blocks, block_width)
    got_count = got_count.reshape(blocks)
    got_slot = got_slot.reshape(blocks)
    capacity = blocks // 2
    live_mask = got_count > 0
    live_rank = jnp.cumsum(live_mask.astype(jnp.int32)) - 1
    compact_pick = live_mask[None, :] & (
        live_rank[None, :] == jnp.arange(capacity, dtype=jnp.int32)[:, None]
    )
    comp_stream = take_blocks(compact_pick, got_stream)
    comp_embed = take_blocks(compact_pick, got_embed)
    comp_count = take_numbers(compact_pick, got_count)
    comp_slot = take_numbers(compact_pick, got_slot)
    slot_pick = comp_slot[:, None] == numbered[None, :]
    comp_cot = take_blocks(slot_pick, cot_blocks)
    compact_rows = capacity * block_rows
    row_counts = jnp.repeat(comp_count, block_rows)
    new_rows, comp_grad = run_core(
        comp_stream.reshape(compact_rows, feature_count),
        comp_embed.reshape(compact_rows, feature_count),
        comp_cot.reshape(compact_rows, feature_count),
        row_counts,
        norm_gain,
        up_parts,
        down_parts,
    )
    spread_pick = slot_pick.T
    place_pick = got_slot[None, :] == numbered[:, None]
    base_stream = take_blocks(place_pick, got_stream)
    live_slot = jnp.any(spread_pick, axis=1)
    spread_stream = take_blocks(spread_pick, new_rows.reshape(capacity, block_width))
    final_stream = jnp.where(live_slot[:, None], spread_stream, base_stream)
    final_grad = take_blocks(spread_pick, comp_grad.reshape(capacity, block_width))
    return (
        final_stream.reshape(row_total, feature_count),
        final_grad.reshape(row_total, feature_count),
    )


def solution(mesh):
    return jax.shard_map(
        shards,
        mesh=mesh,
        in_specs=(
            P("dp", None),
            P("dp", None),
            P("dp", None),
            P(),
            P("dp", "mp"),
            P("mp", "dp"),
            P("dp"),
            P("dp"),
        ),
        out_specs=(P("dp", None), P("dp", None)),
        check_vma=False,
    )
```

```python
import functools

import jax
import jax.numpy as jnp
from jax import lax
from jax.experimental import pallas as pl
from jax.experimental.pallas import tpu as pltpu
from jax.sharding import PartitionSpec as P

EPSILON = 1e-05
MESH = pl.DeviceIdType.MESH


def sum_kernel(n, part_ref, out_ref, got, full, send_sem, recv_sem, share_sem, full_sem):
    me = lax.axis_index("mp")
    barrier = pltpu.get_barrier_semaphore()
    for k in range(1, n):
        peer = lax.rem(me + k, n)
        pl.semaphore_signal(barrier, inc=1, device_id={"mp": peer}, device_id_type=MESH)
    pl.semaphore_wait(barrier, n - 1)
    scatter = []
    for k in range(1, n):
        peer = lax.rem(me + k, n)
        scatter.append(
            pltpu.make_async_remote_copy(
                src_ref=part_ref.at[peer],
                dst_ref=got.at[k],
                send_sem=send_sem.at[k],
                recv_sem=recv_sem.at[k],
                device_id={"mp": peer},
                device_id_type=MESH,
            )
        )
        scatter[-1].start()
    total = part_ref[me].astype(jnp.float32)
    for k in range(1, n):
        scatter[k - 1].wait_recv()
        total = total + got[k].astype(jnp.float32)
    full[0] = total.astype(full.dtype)
    share = []
    for k in range(1, n):
        peer = lax.rem(me + k, n)
        share.append(
            pltpu.make_async_remote_copy(
                src_ref=full.at[0],
                dst_ref=full.at[k],
                send_sem=share_sem.at[k],
                recv_sem=full_sem.at[k],
                device_id={"mp": peer},
                device_id_type=MESH,
            )
        )
        share[-1].start()
    out_ref[me] = full[0]
    for k in range(1, n):
        share[k - 1].wait_recv()
        out_ref[lax.rem(me + n - k, n)] = full[k]
    for k in range(1, n):
        scatter[k - 1].wait_send()
        share[k - 1].wait_send()


def share_kernel(n, own_ref, out_ref, full, send_sem, recv_sem):
    me = lax.axis_index("mp")
    barrier = pltpu.get_barrier_semaphore()
    for k in range(1, n):
        peer = lax.rem(me + k, n)
        pl.semaphore_signal(barrier, inc=1, device_id={"mp": peer}, device_id_type=MESH)
    pl.semaphore_wait(barrier, n - 1)
    share = []
    for k in range(1, n):
        peer = lax.rem(me + k, n)
        share.append(
            pltpu.make_async_remote_copy(
                src_ref=own_ref,
                dst_ref=full.at[k],
                send_sem=send_sem.at[k],
                recv_sem=recv_sem.at[k],
                device_id={"mp": peer},
                device_id_type=MESH,
            )
        )
        share[-1].start()
    out_ref[me] = own_ref[...]
    for k in range(1, n):
        share[k - 1].wait_recv()
        out_ref[lax.rem(me + n - k, n)] = full[k]
    for k in range(1, n):
        share[k - 1].wait_send()


def share_over_mp(value, collective_id):
    n = lax.axis_size("mp")
    if n == 1:
        return value[None]
    shape = (n,) + value.shape
    vmem = pl.BlockSpec(memory_space=pltpu.VMEM)
    return pl.pallas_call(
        functools.partial(share_kernel, n),
        out_shape=jax.ShapeDtypeStruct(shape, value.dtype),
        in_specs=[vmem],
        out_specs=vmem,
        scratch_shapes=[pltpu.VMEM(shape, value.dtype)] + [pltpu.SemaphoreType.DMA((n,))] * 2,
        compiler_params=pltpu.CompilerParams(collective_id=collective_id, has_side_effects=True),
    )(value)


def sum_over_mp(value, collective_id):
    n = lax.axis_size("mp")
    rows, width = value.shape
    if n == 1:
        return value
    each = -(-rows // n)
    padded = jnp.pad(value, ((0, each * n - rows), (0, 0))) if each * n != rows else value
    shape = (n, each, width)
    vmem = pl.BlockSpec(memory_space=pltpu.VMEM)
    out = pl.pallas_call(
        functools.partial(sum_kernel, n),
        out_shape=jax.ShapeDtypeStruct(shape, value.dtype),
        in_specs=[vmem],
        out_specs=vmem,
        scratch_shapes=[pltpu.VMEM(shape, value.dtype)] * 2 + [pltpu.SemaphoreType.DMA((n,))] * 4,
        compiler_params=pltpu.CompilerParams(collective_id=collective_id, has_side_effects=True),
    )(padded.reshape(shape))
    return lax.optimization_barrier(out.reshape(each * n, width)[:rows])


def chunked(value, parts):
    value = lax.optimization_barrier(value)
    return lax.optimization_barrier(value.reshape(value.shape[0], parts, value.shape[1] // parts))


def times_up(value, up_parts):
    return jnp.einsum(
        "rpk,pkf->rf",
        chunked(value, up_parts.shape[0]),
        up_parts,
        preferred_element_type=jnp.float32,
    )


def times_up_transposed(value, up_parts):
    out = jnp.einsum("rf,pkf->rpk", value, up_parts, preferred_element_type=jnp.float32)
    return out.astype(jnp.bfloat16).reshape(value.shape[0], -1)


def times_down(value, down_parts):
    return times_up_transposed(value, down_parts)


def times_down_transposed(value, down_parts):
    return times_up(value, down_parts)


def layer_input(current, embedding, norm_gain):
    values = current.astype(jnp.float32)
    square = jnp.mean(values * values, axis=-1, keepdims=True)
    mixed = values * lax.rsqrt(square + EPSILON) * norm_gain + embedding.astype(jnp.float32)
    return mixed.astype(jnp.bfloat16)


def run_core(current, embedding, cot_rows, row_counts, norm_gain, up_parts, down_parts):
    grad_act = times_down_transposed(cot_rows, down_parts)
    layer_in = layer_input(current, embedding, norm_gain)
    activation = jax.nn.silu(times_up(layer_in, up_parts)).astype(jnp.bfloat16)
    activation = lax.optimization_barrier(activation)
    update = sum_over_mp(times_down(activation, down_parts), 0).astype(jnp.float32)
    advanced = (current.astype(jnp.float32) + update).astype(jnp.bfloat16)
    current = jnp.where((row_counts > 0)[:, None], advanced, current)
    layer_in = layer_input(current, embedding, norm_gain)
    pre_last = times_up(layer_in, up_parts)
    activation = jax.nn.silu(pre_last).astype(jnp.bfloat16)
    sigmoid_pre = jax.nn.sigmoid(pre_last)
    grad_act = lax.optimization_barrier(grad_act)
    grad_pre = (grad_act * (sigmoid_pre * (1.0 + pre_last * (1.0 - sigmoid_pre)))).astype(
        jnp.bfloat16
    )
    both = jnp.concatenate(
        [times_down(activation, down_parts), times_up_transposed(grad_pre, up_parts)], axis=0
    )
    both = sum_over_mp(both, 1)
    update, summed = both[: current.shape[0]], both[current.shape[0] :]
    advanced = (current.astype(jnp.float32) + update.astype(jnp.float32)).astype(jnp.bfloat16)
    last = (row_counts > 1)[:, None]
    return jnp.where(last, advanced, current), jnp.where(last, summed, jnp.zeros_like(summed))


def take_blocks(selector, block_data):
    return jnp.dot(
        selector.astype(jnp.bfloat16), block_data, preferred_element_type=jnp.float32
    ).astype(jnp.bfloat16)


def take_numbers(selector, numbers):
    return jnp.sum(jnp.where(selector, numbers[None, :], 0), axis=1).astype(jnp.int32)


def rows_of(block_numbers, block_rows):
    offsets = jnp.arange(block_rows, dtype=jnp.int32)
    return (block_numbers[:, None] * block_rows + offsets[None, :]).reshape(-1)


def shards(stream, embedding, cotangent, norm_gain, up_weight, down_weight, counts, destination):
    up_parts = lax.all_gather(up_weight, "dp", axis=0, tiled=False)
    down_parts = lax.all_gather(down_weight.T, "dp", axis=0, tiled=False)
    row_total, feature_count = stream.shape
    blocks = counts.shape[0]
    block_rows = row_total // blocks
    peer_count = lax.axis_size("dp")
    per_peer = blocks // peer_count
    capacity = blocks // 2
    numbered = jnp.arange(blocks, dtype=jnp.int32)
    row_numbered = jnp.arange(row_total, dtype=jnp.int32)
    compact_numbered = jnp.arange(capacity * block_rows, dtype=jnp.int32)
    target = destination // blocks
    dest_slot = destination % blocks
    same_target = target[:, None] == target[None, :]
    earlier = numbered[None, :] < numbered[:, None]
    peer_rank = jnp.sum(same_target & earlier, axis=1)
    position = target * per_peer + peer_rank
    send_pick = position[None, :] == numbered[:, None]
    sent_numbers = jnp.stack(
        [
            take_numbers(send_pick, counts).reshape(peer_count, per_peer),
            take_numbers(send_pick, dest_slot).reshape(peer_count, per_peer),
        ],
        axis=1,
    )
    got_numbers = lax.all_to_all(sent_numbers, "dp", split_axis=0, concat_axis=0, tiled=True)
    send_rows = rows_of(position, block_rows)[None, :] == row_numbered[:, None]
    shares = lax.axis_size("mp")
    share = feature_count // shares
    start = lax.axis_index("mp") * share
    own = jnp.concatenate(
        [
            lax.dynamic_slice_in_dim(stream, start, share, axis=1),
            lax.dynamic_slice_in_dim(embedding, start, share, axis=1),
        ],
        axis=1,
    )
    sent = take_blocks(send_rows, own).reshape(peer_count, per_peer * block_rows, 2 * share)
    got = lax.all_to_all(sent, "dp", split_axis=0, concat_axis=0, tiled=True)
    got = share_over_mp(got.reshape(row_total, 2 * share), 2)
    got_stream = jnp.concatenate([got[k, :, :share] for k in range(shares)], axis=1)
    got_embed = jnp.concatenate([got[k, :, share:] for k in range(shares)], axis=1)
    got_count = got_numbers[:, 0, :].reshape(blocks)
    got_slot = got_numbers[:, 1, :].reshape(blocks)
    live_mask = got_count > 0
    live_rank = jnp.cumsum(live_mask.astype(jnp.int32)) - 1
    compact_pick = live_mask[None, :] & (
        live_rank[None, :] == jnp.arange(capacity, dtype=jnp.int32)[:, None]
    )
    comp_count = take_numbers(compact_pick, got_count)
    comp_slot = take_numbers(compact_pick, got_slot)
    compact_at = jnp.where(live_mask, live_rank, capacity)
    compact_rows = rows_of(compact_at, block_rows)[None, :] == compact_numbered[:, None]
    slot_rows = rows_of(comp_slot, block_rows)[:, None] == row_numbered[None, :]
    place_rows = rows_of(got_slot, block_rows)[None, :] == row_numbered[:, None]
    base_stream = lax.optimization_barrier(take_blocks(place_rows, got_stream))
    new_rows, comp_grad = run_core(
        take_blocks(compact_rows, got_stream),
        take_blocks(compact_rows, got_embed),
        take_blocks(slot_rows, cotangent),
        jnp.repeat(comp_count, block_rows),
        norm_gain,
        up_parts,
        down_parts,
    )
    spread_rows = rows_of(comp_slot, block_rows)[None, :] == row_numbered[:, None]
    live_rows = jnp.any(spread_rows, axis=1)
    spread_stream = take_blocks(spread_rows, new_rows)
    final_stream = jnp.where(live_rows[:, None], spread_stream, base_stream)
    return final_stream, take_blocks(spread_rows, comp_grad)


def solution(mesh):
    return jax.shard_map(
        shards,
        mesh=mesh,
        in_specs=(
            P("dp", None),
            P("dp", None),
            P("dp", None),
            P(),
            P("dp", "mp"),
            P("mp", "dp"),
            P("dp"),
            P("dp"),
        ),
        out_specs=(P("dp", None), P("dp", None)),
        check_vma=False,
    )
```

```python
import functools

import jax
import jax.numpy as jnp
from jax import lax
from jax.experimental import pallas as pl
from jax.experimental.pallas import tpu as pltpu
from jax.sharding import PartitionSpec as P

EPSILON = 1e-05
MESH = pl.DeviceIdType.MESH


def sum_kernel(n, part_ref, out_ref, got, full, send_sem, recv_sem, share_sem, full_sem):
    me = lax.axis_index("mp")
    barrier = pltpu.get_barrier_semaphore()
    for k in range(1, n):
        peer = lax.rem(me + k, n)
        pl.semaphore_signal(barrier, inc=1, device_id={"mp": peer}, device_id_type=MESH)
    pl.semaphore_wait(barrier, n - 1)
    scatter = []
    for k in range(1, n):
        peer = lax.rem(me + k, n)
        scatter.append(
            pltpu.make_async_remote_copy(
                src_ref=part_ref.at[peer],
                dst_ref=got.at[k],
                send_sem=send_sem.at[k],
                recv_sem=recv_sem.at[k],
                device_id={"mp": peer},
                device_id_type=MESH,
            )
        )
        scatter[-1].start()
    total = part_ref[me].astype(jnp.float32)
    for k in range(1, n):
        scatter[k - 1].wait_recv()
        total = total + got[k].astype(jnp.float32)
    full[0] = total.astype(full.dtype)
    share = []
    for k in range(1, n):
        peer = lax.rem(me + k, n)
        share.append(
            pltpu.make_async_remote_copy(
                src_ref=full.at[0],
                dst_ref=full.at[k],
                send_sem=share_sem.at[k],
                recv_sem=full_sem.at[k],
                device_id={"mp": peer},
                device_id_type=MESH,
            )
        )
        share[-1].start()
    out_ref[me] = full[0]
    for k in range(1, n):
        share[k - 1].wait_recv()
        out_ref[lax.rem(me + n - k, n)] = full[k]
    for k in range(1, n):
        scatter[k - 1].wait_send()
        share[k - 1].wait_send()


def share_kernel(n, own_ref, out_ref, full, send_sem, recv_sem):
    me = lax.axis_index("mp")
    barrier = pltpu.get_barrier_semaphore()
    for k in range(1, n):
        peer = lax.rem(me + k, n)
        pl.semaphore_signal(barrier, inc=1, device_id={"mp": peer}, device_id_type=MESH)
    pl.semaphore_wait(barrier, n - 1)
    share = []
    for k in range(1, n):
        peer = lax.rem(me + k, n)
        share.append(
            pltpu.make_async_remote_copy(
                src_ref=own_ref,
                dst_ref=full.at[k],
                send_sem=send_sem.at[k],
                recv_sem=recv_sem.at[k],
                device_id={"mp": peer},
                device_id_type=MESH,
            )
        )
        share[-1].start()
    out_ref[me] = own_ref[...]
    for k in range(1, n):
        share[k - 1].wait_recv()
        out_ref[lax.rem(me + n - k, n)] = full[k]
    for k in range(1, n):
        share[k - 1].wait_send()


def share_over_mp(value, collective_id):
    n = lax.axis_size("mp")
    if n == 1:
        return value[None]
    shape = (n,) + value.shape
    vmem = pl.BlockSpec(memory_space=pltpu.VMEM)
    return pl.pallas_call(
        functools.partial(share_kernel, n),
        out_shape=jax.ShapeDtypeStruct(shape, value.dtype),
        in_specs=[vmem],
        out_specs=vmem,
        scratch_shapes=[pltpu.VMEM(shape, value.dtype)] + [pltpu.SemaphoreType.DMA((n,))] * 2,
        compiler_params=pltpu.CompilerParams(collective_id=collective_id, has_side_effects=True),
    )(value)


def sum_over_mp(value, collective_id):
    n = lax.axis_size("mp")
    rows, width = value.shape
    if n == 1:
        return value
    each = -(-rows // n)
    padded = jnp.pad(value, ((0, each * n - rows), (0, 0))) if each * n != rows else value
    shape = (n, each, width)
    vmem = pl.BlockSpec(memory_space=pltpu.VMEM)
    out = pl.pallas_call(
        functools.partial(sum_kernel, n),
        out_shape=jax.ShapeDtypeStruct(shape, value.dtype),
        in_specs=[vmem],
        out_specs=vmem,
        scratch_shapes=[pltpu.VMEM(shape, value.dtype)] * 2 + [pltpu.SemaphoreType.DMA((n,))] * 4,
        compiler_params=pltpu.CompilerParams(collective_id=collective_id, has_side_effects=True),
    )(padded.reshape(shape))
    return lax.optimization_barrier(out.reshape(each * n, width)[:rows])


def chunked(value, parts):
    value = lax.optimization_barrier(value)
    return lax.optimization_barrier(value.reshape(value.shape[0], parts, value.shape[1] // parts))


def times_up(value, up_parts):
    return jnp.einsum(
        "rpk,pkf->rf",
        chunked(value, up_parts.shape[0]),
        up_parts,
        preferred_element_type=jnp.float32,
    )


def times_up_transposed(value, up_parts):
    out = jnp.einsum("rf,pkf->rpk", value, up_parts, preferred_element_type=jnp.float32)
    return out.astype(jnp.bfloat16).reshape(value.shape[0], -1)


def times_down(value, down_parts):
    return times_up_transposed(value, down_parts)


def times_down_transposed(value, down_parts):
    return times_up(value, down_parts)


def swap(value):
    size = lax.axis_size("dp")
    pairs = [(index, (index + size // 2) % size) for index in range(size)]
    return lax.ppermute(value, "dp", pairs)


def swap_sum(partial_value, own_rows):
    other = swap(partial_value[own_rows:].astype(jnp.bfloat16))
    return partial_value[:own_rows] + other.astype(jnp.float32)


def both_rows(own):
    return jnp.concatenate([own, swap(own)], axis=0)


def layer_input(current, embedding, gain, own_rows, width):
    values = current.astype(jnp.float32)
    square = jnp.sum(values * values, axis=-1)
    other = swap(square)
    square = square + jnp.concatenate([other[own_rows:], other[:own_rows]])
    scale = lax.rsqrt(square / width + EPSILON)[:, None]
    mixed = values * scale * gain + embedding.astype(jnp.float32)
    return mixed.astype(jnp.bfloat16)


def run_core(current, embedding, cot_rows, row_counts, gain, width, up_parts, down_parts):
    own_rows = current.shape[0] // 2
    layer_in = layer_input(current, embedding, gain, own_rows, width)
    pre_act = swap_sum(times_up(layer_in, up_parts), own_rows)
    activation = both_rows(jax.nn.silu(pre_act).astype(jnp.bfloat16))
    grad_act = swap_sum(times_down_transposed(cot_rows, down_parts), own_rows)
    update = sum_over_mp(times_down(activation, down_parts), 0).astype(jnp.float32)
    advanced = (current.astype(jnp.float32) + update).astype(jnp.bfloat16)
    current = jnp.where((row_counts > 0)[:, None], advanced, current)
    layer_in = layer_input(current, embedding, gain, own_rows, width)
    pre_last = swap_sum(times_up(layer_in, up_parts), own_rows)
    sigmoid_pre = jax.nn.sigmoid(pre_last)
    activation = both_rows((pre_last * sigmoid_pre).astype(jnp.bfloat16))
    grad_pre = (grad_act * (sigmoid_pre * (1.0 + pre_last * (1.0 - sigmoid_pre)))).astype(
        jnp.bfloat16
    )
    grad_pre = both_rows(grad_pre)
    both = jnp.concatenate(
        [times_down(activation, down_parts), times_up_transposed(grad_pre, up_parts)], axis=0
    )
    both = sum_over_mp(both, 1)
    update, summed = both[: 2 * own_rows], both[2 * own_rows :]
    advanced = (current.astype(jnp.float32) + update.astype(jnp.float32)).astype(jnp.bfloat16)
    last = (row_counts > 1)[:, None]
    return jnp.where(last, advanced, current), jnp.where(last, summed, jnp.zeros_like(summed))


def take_blocks(selector, block_data):
    return jnp.dot(
        selector.astype(jnp.bfloat16), block_data, preferred_element_type=jnp.float32
    ).astype(jnp.bfloat16)


def take_numbers(selector, numbers):
    return jnp.sum(jnp.where(selector, numbers[None, :], 0), axis=1).astype(jnp.int32)


def rows_of(block_numbers, block_rows):
    offsets = jnp.arange(block_rows, dtype=jnp.int32)
    return (block_numbers[:, None] * block_rows + offsets[None, :]).reshape(-1)


def for_pairs(value, halves=None):
    half_size = value.shape[0] // 2
    sides = value.reshape((2, half_size) + value.shape[1:])
    picked = []
    for side in range(2):
        own, other = sides[side], sides[1 - side]
        if halves is not None:
            own, other = own[:, :, side], other[:, :, side]
        picked.append(jnp.stack([own, other], axis=1))
    return jnp.concatenate(picked, axis=0)


def shards(stream, embedding, cotangent, norm_gain, up_weight, down_weight, counts, destination):
    peer_count = lax.axis_size("dp")
    half_peers = peer_count // 2
    groups = [list(range(half_peers)), list(range(half_peers, peer_count))]
    up_parts = lax.all_gather(up_weight, "dp", axis=0, tiled=False, axis_index_groups=groups)
    down_parts = lax.all_gather(down_weight.T, "dp", axis=0, tiled=False, axis_index_groups=groups)
    first = lax.axis_index("dp") < half_peers
    row_total, feature_count = stream.shape
    half = feature_count // 2
    blocks = counts.shape[0]
    block_rows = row_total // blocks
    per_peer = blocks // peer_count
    capacity = blocks // 2
    numbered = jnp.arange(blocks, dtype=jnp.int32)
    row_numbered = jnp.arange(row_total, dtype=jnp.int32)
    compact_numbered = jnp.arange(capacity * block_rows, dtype=jnp.int32)
    target = destination // blocks
    dest_slot = destination % blocks
    same_target = target[:, None] == target[None, :]
    earlier = numbered[None, :] < numbered[:, None]
    peer_rank = jnp.sum(same_target & earlier, axis=1)
    position = target * per_peer + peer_rank
    send_pick = position[None, :] == numbered[:, None]
    sent_numbers = jnp.stack(
        [
            take_numbers(send_pick, counts).reshape(peer_count, per_peer),
            take_numbers(send_pick, dest_slot).reshape(peer_count, per_peer),
        ],
        axis=1,
    )
    got_numbers = lax.all_to_all(
        for_pairs(sent_numbers), "dp", split_axis=0, concat_axis=0, tiled=True
    )
    send_rows = rows_of(position, block_rows)[None, :] == row_numbered[:, None]
    shares = lax.axis_size("mp")
    share = -(-half // shares)
    start = lax.axis_index("mp") * share

    def own_share(value):
        sides = [value[:, :half], value[:, half:]]
        sides = [jnp.pad(side, ((0, 0), (0, share * shares - half))) for side in sides]
        return [lax.dynamic_slice_in_dim(side, start, share, axis=1) for side in sides]

    own_stream, own_embed = own_share(stream), own_share(embedding)
    own = jnp.concatenate([own_stream[0], own_embed[0], own_stream[1], own_embed[1]], axis=1)
    peer_rows = per_peer * block_rows
    sent = take_blocks(send_rows, own).reshape(peer_count, peer_rows, 2, 2 * share)
    got = lax.all_to_all(
        for_pairs(sent, 2), "dp", split_axis=0, concat_axis=0, tiled=True
    )
    got = got.transpose(1, 0, 2, 3).reshape(2 * row_total, 2 * share)
    got = share_over_mp(got, 2)
    got_stream = jnp.concatenate([got[k, :, :share] for k in range(shares)], axis=1)[:, :half]
    got_embed = jnp.concatenate([got[k, :, share:] for k in range(shares)], axis=1)[:, :half]

    def full_width(own_half, other_half):
        left = jnp.where(first, own_half, other_half)
        right = jnp.where(first, other_half, own_half)
        return jnp.concatenate([left, right], axis=1)

    streams, embeds, row_counts, slots = [], [], [], []
    for side in range(2):
        got_count = got_numbers[:, side, 0, :].reshape(blocks)
        got_slot = got_numbers[:, side, 1, :].reshape(blocks)
        live_mask = got_count > 0
        live_rank = jnp.cumsum(live_mask.astype(jnp.int32)) - 1
        compact_pick = live_mask[None, :] & (
            live_rank[None, :] == jnp.arange(capacity, dtype=jnp.int32)[:, None]
        )
        compact_at = jnp.where(live_mask, live_rank, capacity)
        compact_rows = rows_of(compact_at, block_rows)[None, :] == compact_numbered[:, None]
        side_rows = slice(side * row_total, (side + 1) * row_total)
        streams.append(take_blocks(compact_rows, got_stream[side_rows]))
        embeds.append(take_blocks(compact_rows, got_embed[side_rows]))
        row_counts.append(jnp.repeat(take_numbers(compact_pick, got_count), block_rows))
        slots.append((take_numbers(compact_pick, got_slot), got_slot))
    comp_slot, got_slot = slots[0]
    slot_rows = rows_of(comp_slot, block_rows)[:, None] == row_numbered[None, :]
    place_rows = rows_of(got_slot, block_rows)[None, :] == row_numbered[:, None]
    comp_cot = take_blocks(slot_rows, cotangent)
    left_cot, right_cot = comp_cot[:, :half], comp_cot[:, half:]
    own_cot = jnp.where(first, left_cot, right_cot)
    other_cot = swap(jnp.where(first, right_cot, left_cot))
    arrived = full_width(got_stream[:row_total], swap(got_stream[row_total:]))
    base_stream = lax.optimization_barrier(take_blocks(place_rows, arrived))
    gain = jnp.where(first, norm_gain[:half], norm_gain[half:])
    new_rows, comp_grad = run_core(
        jnp.concatenate(streams, axis=0),
        jnp.concatenate(embeds, axis=0),
        jnp.concatenate([own_cot, other_cot], axis=0),
        jnp.concatenate(row_counts, axis=0),
        gain,
        feature_count,
        up_parts,
        down_parts,
    )
    own_rows = capacity * block_rows
    other = swap(jnp.concatenate([new_rows[own_rows:], comp_grad[own_rows:]], axis=0))
    new_rows = full_width(new_rows[:own_rows], other[:own_rows])
    comp_grad = full_width(comp_grad[:own_rows], other[own_rows:])
    spread_rows = rows_of(comp_slot, block_rows)[None, :] == row_numbered[:, None]
    live_rows = jnp.any(spread_rows, axis=1)
    spread_stream = take_blocks(spread_rows, new_rows)
    final_stream = jnp.where(live_rows[:, None], spread_stream, base_stream)
    return final_stream, take_blocks(spread_rows, comp_grad)


def solution(mesh):
    return jax.shard_map(
        shards,
        mesh=mesh,
        in_specs=(
            P("dp", None),
            P("dp", None),
            P("dp", None),
            P(),
            P("dp", "mp"),
            P("mp", "dp"),
            P("dp"),
            P("dp"),
        ),
        out_specs=(P("dp", None), P("dp", None)),
        check_vma=False,
    )
```

```python
import functools

import jax
import jax.numpy as jnp
from jax import lax
from jax.experimental import pallas as pl
from jax.experimental.pallas import tpu as pltpu
from jax.sharding import PartitionSpec as P


EPSILON = 1e-05
MESH = pl.DeviceIdType.MESH


def sum_kernel(n, part_ref, out_ref, got, full, send_sem, recv_sem, share_sem, full_sem):
    me = lax.axis_index("mp")
    barrier = pltpu.get_barrier_semaphore()
    for k in range(1, n):
        peer = lax.rem(me + k, n)
        pl.semaphore_signal(barrier, inc=1, device_id={"mp": peer}, device_id_type=MESH)
    pl.semaphore_wait(barrier, n - 1)
    scatter = []
    for k in range(1, n):
        peer = lax.rem(me + k, n)
        scatter.append(
            pltpu.make_async_remote_copy(
                src_ref=part_ref.at[peer],
                dst_ref=got.at[k],
                send_sem=send_sem.at[k],
                recv_sem=recv_sem.at[k],
                device_id={"mp": peer},
                device_id_type=MESH,
            )
        )
        scatter[-1].start()
    total = part_ref[me].astype(jnp.float32)
    for k in range(1, n):
        scatter[k - 1].wait_recv()
        total = total + got[k].astype(jnp.float32)
    full[0] = total.astype(full.dtype)
    share = []
    for k in range(1, n):
        peer = lax.rem(me + k, n)
        share.append(
            pltpu.make_async_remote_copy(
                src_ref=full.at[0],
                dst_ref=full.at[k],
                send_sem=share_sem.at[k],
                recv_sem=full_sem.at[k],
                device_id={"mp": peer},
                device_id_type=MESH,
            )
        )
        share[-1].start()
    out_ref[me] = full[0]
    for k in range(1, n):
        share[k - 1].wait_recv()
        out_ref[lax.rem(me + n - k, n)] = full[k]
    for k in range(1, n):
        scatter[k - 1].wait_send()
        share[k - 1].wait_send()


def share_kernel(n, own_ref, out_ref, full, send_sem, recv_sem):
    me = lax.axis_index("mp")
    barrier = pltpu.get_barrier_semaphore()
    for k in range(1, n):
        peer = lax.rem(me + k, n)
        pl.semaphore_signal(barrier, inc=1, device_id={"mp": peer}, device_id_type=MESH)
    pl.semaphore_wait(barrier, n - 1)
    share = []
    for k in range(1, n):
        peer = lax.rem(me + k, n)
        share.append(
            pltpu.make_async_remote_copy(
                src_ref=own_ref,
                dst_ref=full.at[k],
                send_sem=send_sem.at[k],
                recv_sem=recv_sem.at[k],
                device_id={"mp": peer},
                device_id_type=MESH,
            )
        )
        share[-1].start()
    out_ref[me] = own_ref[...]
    for k in range(1, n):
        share[k - 1].wait_recv()
        out_ref[lax.rem(me + n - k, n)] = full[k]
    for k in range(1, n):
        share[k - 1].wait_send()


def share_over_mp(value, collective_id):
    n = lax.axis_size("mp")
    if n == 1:
        return value[None]
    shape = (n,) + value.shape
    vmem = pl.BlockSpec(memory_space=pltpu.VMEM)
    return pl.pallas_call(
        functools.partial(share_kernel, n),
        out_shape=jax.ShapeDtypeStruct(shape, value.dtype),
        in_specs=[vmem],
        out_specs=vmem,
        scratch_shapes=[pltpu.VMEM(shape, value.dtype)] + [pltpu.SemaphoreType.DMA((n,))] * 2,
        compiler_params=pltpu.CompilerParams(collective_id=collective_id, has_side_effects=True),
    )(value)


def sum_over_mp(value, collective_id):
    n = lax.axis_size("mp")
    rows, width = value.shape
    if n == 1:
        return value
    each = -(-rows // n)
    padded = jnp.pad(value, ((0, each * n - rows), (0, 0))) if each * n != rows else value
    shape = (n, each, width)
    vmem = pl.BlockSpec(memory_space=pltpu.VMEM)
    out = pl.pallas_call(
        functools.partial(sum_kernel, n),
        out_shape=jax.ShapeDtypeStruct(shape, value.dtype),
        in_specs=[vmem],
        out_specs=vmem,
        cost_estimate=pl.CostEstimate(
            flops=0, bytes_accessed=160 * value.size * value.dtype.itemsize, transcendentals=0
        ),
        scratch_shapes=[pltpu.VMEM(shape, value.dtype)] * 2 + [pltpu.SemaphoreType.DMA((n,))] * 4,
        compiler_params=pltpu.CompilerParams(collective_id=collective_id, has_side_effects=True),
    )(padded.reshape(shape))
    return lax.optimization_barrier(out.reshape(each * n, width)[:rows])


def chunked(value, parts):
    value = lax.optimization_barrier(value)
    return lax.optimization_barrier(value.reshape(value.shape[0], parts, value.shape[1] // parts))


def times_up(value, up_parts):
    return jnp.einsum(
        "rpk,pkf->rf",
        chunked(value, up_parts.shape[0]),
        up_parts,
        preferred_element_type=jnp.float32,
    )


def times_up_transposed(value, up_parts):
    out = jnp.einsum("rf,pkf->rpk", value, up_parts, preferred_element_type=jnp.float32)
    return out.astype(jnp.bfloat16).reshape(value.shape[0], -1)


def times_down(value, down_parts):
    return times_up_transposed(value, down_parts)


def times_down_transposed(value, down_parts):
    return times_up(value, down_parts)


def swap(value):
    size = lax.axis_size("dp")
    pairs = [(index, (index + size // 2) % size) for index in range(size)]
    return lax.ppermute(value, "dp", pairs)


def swap_sum(partial_value, own_rows):
    other = swap(partial_value.astype(jnp.bfloat16))
    other = jnp.concatenate([other[own_rows:], other[:own_rows]], axis=0)
    return partial_value + other.astype(jnp.float32)


def layer_input(current, embedding, gain, own_rows, width):
    values = current.astype(jnp.float32)
    square = jnp.sum(values * values, axis=-1)
    other = swap(square)
    square = square + jnp.concatenate([other[own_rows:], other[:own_rows]])
    scale = lax.rsqrt(square / width + EPSILON)[:, None]
    mixed = values * scale * gain + embedding.astype(jnp.float32)
    return mixed.astype(jnp.bfloat16)


def run_core(current, embedding, cot_rows, row_counts, gain, width, up_parts, down_parts, passed):
    own_rows = current.shape[0] // 2
    layer_in = layer_input(current, embedding, gain, own_rows, width)
    pre_act = swap_sum(times_up(layer_in, up_parts), own_rows)
    activation = lax.optimization_barrier(jax.nn.silu(pre_act).astype(jnp.bfloat16))
    grad_part = times_down_transposed(cot_rows, down_parts)
    activation, grad_part = lax.optimization_barrier((activation, grad_part))
    update_part = times_down(activation, down_parts)
    grad_act = swap_sum(grad_part, own_rows)
    update = sum_over_mp(update_part, 0)
    update = update.astype(jnp.float32)
    advanced = (current.astype(jnp.float32) + update).astype(jnp.bfloat16)
    current = jnp.where((row_counts > 0)[:, None], advanced, current)
    layer_in = layer_input(current, embedding, gain, own_rows, width)
    pre_last = swap_sum(times_up(layer_in, up_parts), own_rows)
    sigmoid_pre = jax.nn.sigmoid(pre_last)
    activation = (pre_last * sigmoid_pre).astype(jnp.bfloat16)
    grad_pre = (grad_act * (sigmoid_pre * (1.0 + pre_last * (1.0 - sigmoid_pre)))).astype(
        jnp.bfloat16
    )
    activation, grad_pre = lax.optimization_barrier((activation, grad_pre))
    both = jnp.concatenate(
        [times_down(activation, down_parts), times_up_transposed(grad_pre, up_parts)], axis=0
    )
    both, passed = lax.optimization_barrier((both, passed))
    passed = swap(passed)
    both = sum_over_mp(both, 1)
    update, summed = both[: 2 * own_rows], both[2 * own_rows :]
    advanced = (current.astype(jnp.float32) + update.astype(jnp.float32)).astype(jnp.bfloat16)
    last = (row_counts > 1)[:, None]
    new_rows = jnp.where(last, advanced, current)
    return new_rows, jnp.where(last, summed, jnp.zeros_like(summed)), passed


def take_blocks(selector, block_data):
    return jnp.dot(
        selector.astype(jnp.bfloat16), block_data, preferred_element_type=jnp.float32
    ).astype(jnp.bfloat16)


def take_numbers(selector, numbers):
    return jnp.sum(jnp.where(selector, numbers[None, :], 0), axis=1).astype(jnp.int32)


def rows_of(block_numbers, block_rows):
    offsets = jnp.arange(block_rows, dtype=jnp.int32)
    return (block_numbers[:, None] * block_rows + offsets[None, :]).reshape(-1)


def for_pairs(value, halves=None):
    half_size = value.shape[0] // 2
    sides = value.reshape((2, half_size) + value.shape[1:])
    picked = []
    for side in range(2):
        own, other = sides[side], sides[1 - side]
        if halves is not None:
            own, other = own[:, :, side], other[:, :, side]
        picked.append(jnp.stack([own, other], axis=1))
    return jnp.concatenate(picked, axis=0)


def shards(stream, embedding, cotangent, norm_gain, up_weight, down_weight, counts, destination):
    peer_count = lax.axis_size("dp")
    half_peers = peer_count // 2
    groups = [list(range(half_peers)), list(range(half_peers, peer_count))]
    up_parts = lax.all_gather(up_weight, "dp", axis=0, tiled=False, axis_index_groups=groups)
    down_parts = lax.all_gather(down_weight.T, "dp", axis=0, tiled=False, axis_index_groups=groups)
    first = lax.axis_index("dp") < half_peers
    row_total, feature_count = stream.shape
    half = feature_count // 2
    blocks = counts.shape[0]
    block_rows = row_total // blocks
    per_peer = blocks // peer_count
    capacity = blocks // 2
    numbered = jnp.arange(blocks, dtype=jnp.int32)
    row_numbered = jnp.arange(row_total, dtype=jnp.int32)
    compact_numbered = jnp.arange(capacity * block_rows, dtype=jnp.int32)
    target = destination // blocks
    dest_slot = destination % blocks
    same_target = target[:, None] == target[None, :]
    earlier = numbered[None, :] < numbered[:, None]
    peer_rank = jnp.sum(same_target & earlier, axis=1)
    position = target * per_peer + peer_rank
    send_pick = position[None, :] == numbered[:, None]
    sent_numbers = jnp.stack(
        [
            take_numbers(send_pick, counts).reshape(peer_count, per_peer),
            take_numbers(send_pick, dest_slot).reshape(peer_count, per_peer),
        ],
        axis=1,
    )
    got_numbers = lax.all_to_all(
        for_pairs(sent_numbers), "dp", split_axis=0, concat_axis=0, tiled=True
    )
    send_rows = rows_of(position, block_rows)[None, :] == row_numbered[:, None]
    shares = lax.axis_size("mp")
    share = -(-half // shares)
    start = lax.axis_index("mp") * share

    def own_share(value):
        sides = [value[:, :half], value[:, half:]]
        sides = [jnp.pad(side, ((0, 0), (0, share * shares - half))) for side in sides]
        return [lax.dynamic_slice_in_dim(side, start, share, axis=1) for side in sides]

    own_stream, own_embed = own_share(stream), own_share(embedding)
    own = jnp.concatenate([own_stream[0], own_embed[0], own_stream[1], own_embed[1]], axis=1)
    peer_rows = per_peer * block_rows
    sent = take_blocks(send_rows, own).reshape(peer_count, peer_rows, 2, 2 * share)
    got = lax.all_to_all(
        for_pairs(sent, 2), "dp", split_axis=0, concat_axis=0, tiled=True
    )
    got = got.transpose(1, 0, 2, 3).reshape(2 * row_total, 2 * share)
    got = share_over_mp(got, 2)
    got_stream = jnp.concatenate([got[k, :, :share] for k in range(shares)], axis=1)[:, :half]
    got_embed = jnp.concatenate([got[k, :, share:] for k in range(shares)], axis=1)[:, :half]

    def full_width(own_half, other_half):
        left = jnp.where(first, own_half, other_half)
        right = jnp.where(first, other_half, own_half)
        return jnp.concatenate([left, right], axis=1)

    streams, embeds, row_counts, slots = [], [], [], []
    for side in range(2):
        got_count = got_numbers[:, side, 0, :].reshape(blocks)
        got_slot = got_numbers[:, side, 1, :].reshape(blocks)
        live_mask = got_count > 0
        live_rank = jnp.cumsum(live_mask.astype(jnp.int32)) - 1
        compact_pick = live_mask[None, :] & (
            live_rank[None, :] == jnp.arange(capacity, dtype=jnp.int32)[:, None]
        )
        compact_at = jnp.where(live_mask, live_rank, capacity)
        compact_rows = rows_of(compact_at, block_rows)[None, :] == compact_numbered[:, None]
        side_rows = slice(side * row_total, (side + 1) * row_total)
        streams.append(take_blocks(compact_rows, got_stream[side_rows]))
        embeds.append(take_blocks(compact_rows, got_embed[side_rows]))
        row_counts.append(jnp.repeat(take_numbers(compact_pick, got_count), block_rows))
        slots.append((take_numbers(compact_pick, got_slot), got_slot))
    comp_slot, got_slot = slots[0]
    slot_rows = rows_of(comp_slot, block_rows)[:, None] == row_numbered[None, :]
    place_rows = rows_of(got_slot, block_rows)[None, :] == row_numbered[:, None]
    comp_cot = take_blocks(slot_rows, cotangent)
    left_cot, right_cot = comp_cot[:, :half], comp_cot[:, half:]
    own_cot = jnp.where(first, left_cot, right_cot)
    other_cot = swap(jnp.where(first, right_cot, left_cot))
    gain = jnp.where(first, norm_gain[:half], norm_gain[half:])
    new_rows, comp_grad, arrived = run_core(
        jnp.concatenate(streams, axis=0),
        jnp.concatenate(embeds, axis=0),
        jnp.concatenate([own_cot, other_cot], axis=0),
        jnp.concatenate(row_counts, axis=0),
        gain,
        feature_count,
        up_parts,
        down_parts,
        got_stream[row_total:],
    )
    base_stream = take_blocks(place_rows, full_width(got_stream[:row_total], arrived))
    own_rows = capacity * block_rows
    other = swap(jnp.concatenate([new_rows[own_rows:], comp_grad[own_rows:]], axis=0))
    new_rows = full_width(new_rows[:own_rows], other[:own_rows])
    comp_grad = full_width(comp_grad[:own_rows], other[own_rows:])
    spread_rows = rows_of(comp_slot, block_rows)[None, :] == row_numbered[:, None]
    live_rows = jnp.any(spread_rows, axis=1)
    spread_stream = take_blocks(spread_rows, new_rows)
    final_stream = jnp.where(live_rows[:, None], spread_stream, base_stream)
    return final_stream, take_blocks(spread_rows, comp_grad)


def solution(mesh):
    return jax.shard_map(
        shards,
        mesh=mesh,
        in_specs=(
            P("dp", None),
            P("dp", None),
            P("dp", None),
            P(),
            P("dp", "mp"),
            P("mp", "dp"),
            P("dp"),
            P("dp"),
        ),
        out_specs=(P("dp", None), P("dp", None)),
        check_vma=False,
    )
```
